32 devices in a mesh: parts: 2 (over x), ep: 16 (over z, y, core), mem: 1.
Axes of the slice: x: 2, y: 2, z: 4, core: 2. Of those that a mesh axis runs over, the one named last changes fastest.
Arguments:
- saved_inputs: bfloat16 [4096, 2048], P(('parts', 'ep'), 'mem'), parts along dimension 0, may hold values from -6 to 6
- out_grads: bfloat16 [4096, 2048], P(('parts', 'ep'), 'mem'), parts along dimension 0, may hold values from -6 to 6
- expert_ids: int32 [4096, 8], P(('parts', 'ep')), parts along dimension 0, may hold values from 0 to 15, all different within a row; in each aligned block of 128 rows (0 to 127, 128 to 255, ...) at most 72 rows name the same one
- gate_weights: float32 [4096, 8], P(('parts', 'ep')), parts along dimension 0, may hold values from 0.05 to 0.5
- gate_up: bfloat16 [32, 2, 384, 2048], P(('parts', 'ep'), None, 'mem'), parts along dimension 0, may hold values from -0.125 to 0.125
- down_proj: bfloat16 [32, 384, 2048], P(('parts', 'ep'), 'mem'), parts along dimension 0, may hold values from -0.3125 to 0.3125
- owner_before: int32 [32], P('parts'), parts along dimension 0, may hold values from 0 to 15, each once
- migrating: int32 [16], P('parts'), parts along dimension 0, may hold values from 0 to 15, as said below
Outputs:
- input_grads: bfloat16 [4096, 2048], P(('parts', 'ep'), 'mem'), parts along dimension 0
- moved_gate_up: bfloat16 [32, 2, 384, 2048], P(('parts', 'ep'), None, 'mem'), parts along dimension 0
- moved_down: bfloat16 [32, 384, 2048], P(('parts', 'ep'), 'mem'), parts along dimension 0
- gate_up_grads: float32 [32, 2, 384, 2048], P(('parts', 'ep'), None, 'mem'), parts along dimension 0
- down_grads: float32 [32, 384, 2048], P(('parts', 'ep'), 'mem'), parts along dimension 0
The draws below stay inside these ranges and needn't reach their ends.
There are 2 independent parts, one for each index of `parts`. The reference program is written for one: setup_inputs(seed, part) draws one part's arguments, and reference() takes and returns one part's arrays. A program takes and returns all parts, laid end to end along the dimension named above; each array names one. Nothing has to cross between parts.
Inputs may be any that keep to these rules, and one draw needn't show every extreme that they name: `expert_ids`: each row names 8 different experts; in each aligned block of 128 rows (the rows of one index of ep) no expert is named more than 72 times, and in some blocks one is named exactly 72 times. `owner_before`: a permutation: every owner index holds one expert. `migrating`: 8 distinct experts.
All inputs are finite; a program needn't handle non-finite values.
Results may differ from the reference program's by a relative error of at most 0.012.
Values may be sent and summed in bfloat16 or wider, within the bound.
No kernel may reach another device: no remote copies, remote signals or barrier semaphores. Data moves between devices by JAX's collectives and lax.ppermute only.
A program may use at most 128 MiB of HBM per device.

```python
import math
import jax
import jax.numpy as jnp
import numpy as np
from jax import lax

D = 2048
HIDDEN_SIZE = 384
TOP = 8
TOK = 128
EXPERTS = 16
TOKENS = 2048
CAP = 72
MIGRATE = 8
N_EP = 16
N_MEM = 1


def draw_migrating(key, part):
    order = jax.random.permutation(key, EXPERTS)
    return order[:MIGRATE].astype(jnp.int32)


def level_of(key, shape, shards, smallest, high):
    loudness = 1.0
    for axis_at, parts in shards:
        steps = jax.random.uniform(jax.random.fold_in(jax.random.fold_in(key, 6), axis_at), (parts,), jnp.float32, smallest / len(shards), high / len(shards))
        loudness = loudness * jnp.repeat(jnp.exp(steps), shape[axis_at] // parts).reshape((-1,) + (1,) * (len(shape) - 1 - axis_at))
    return loudness


def routed_block(key, own, number, rows, number_of, top, reach, lean):
    order = jax.random.permutation(key, number_of)
    crowded, ordinary = shares(number_of, rows * top, reach, lean, True), shares(number_of, rows * top, reach, lean, False)
    places = jnp.arange(number_of)

    def named(tallies, turn):
        used = int((tallies > 0).sum())
        fixed = max(1, used // 4)
        passed = fixed + (places - fixed + turn * (used - fixed)) % max(1, number_of - fixed)
        return jnp.zeros((number_of,), jnp.int32).at[order[jnp.where(places < fixed, places, passed)]].set(jnp.asarray(tallies, jnp.int32))

    tallies = jnp.where(number % 4 == 0, named(crowded, number // 4), named(ordinary, number - number // 4 - 1))
    mixed = jax.random.permutation(jax.random.fold_in(own, 3), number_of)
    giver, taker = mixed[0:number_of // 2 * 2:2], mixed[1:number_of // 2 * 2:2]
    room = jnp.minimum(tallies[giver] - 1, reach - tallies[taker]) // 2
    room = jnp.where((giver == order[0]) | (taker == order[0]) | (tallies[taker] == 0), 0, jnp.maximum(room, 0))
    passed = jax.random.randint(jax.random.fold_in(own, 4), (number_of // 2,), 0, 1 << 20) % (room + 1)
    tallies = tallies.at[giver].add(-passed).at[taker].add(passed)
    labels = jnp.searchsorted(jnp.cumsum(tallies), jnp.arange(rows * top), side="right").astype(jnp.int32)
    grid = labels.reshape(top, rows).T
    grid = grid[jax.random.permutation(jax.random.fold_in(own, 1), rows)]
    turn = jax.random.randint(jax.random.fold_in(own, 2), (rows, 1), 0, top)
    return jnp.take_along_axis(grid, (jnp.arange(top)[None, :] + turn) % top, axis=1)


def shares(count, total, bound, skew, full):
    portions = [(1 << 20) // math.isqrt(standing ** skew) + 1 for standing in range(1, count + 1)]
    largest = bound if full else min(bound, max(-(-total // count), total * portions[0] // sum(portions)))
    least = 1 if total - largest >= count - 1 else 0
    holding, spare = [largest] + [least] * (count - 1), total - largest - least * (count - 1)
    while spare > 0:
        candidates = [i for i in range(1, count) if holding[i] < largest] or [i for i in range(1, count) if holding[i] < bound]
        mass, remaining = sum([portions[i] for i in candidates]), spare
        for i in candidates:
            more = min(bound - holding[i], max(1, remaining * portions[i] // mass), spare)
            holding[i] = holding[i] + more
            spare = spare - more
    return np.array(holding)


def centred(stream_key, dims, spread, bound, cuts=(), kind=jnp.bfloat16):
    array = jax.random.normal(stream_key, dims, jnp.float32) * spread
    if len(cuts) > 0:
        array = level_of(stream_key, dims, cuts, -0.22, 0.18) * array
    return jnp.clip(array, min=-bound, max=bound).astype(kind)


def setup_inputs(seed: int = 0, part: int = 0) -> dict:
    arg_keys = jax.random.split(jax.random.key(seed), 9)
    own_keys = jax.random.split(jax.random.fold_in(arg_keys[8], part), 9)
    saved_inputs = centred(own_keys[0], (TOKENS, D), 1.0, 6.0, ((0, 16),))
    out_grads = centred(own_keys[1], (TOKENS, D), 1.0, 6.0, ((0, 16),))
    expert_ids_keys = jax.random.split(jax.random.fold_in(own_keys[2], 1), TOKENS // TOK)
    expert_ids_turns = jax.random.permutation(jax.random.fold_in(own_keys[2], 3), TOKENS // TOK)
    expert_ids = jax.vmap(lambda own, number: routed_block(jax.random.fold_in(own_keys[2], 2), own, number, TOK, EXPERTS, TOP, CAP, 2))(expert_ids_keys, expert_ids_turns).reshape((TOKENS, TOP))
    gate_weights = jnp.clip(jnp.exp(math.log(0.5) - 2.3025851 * jax.random.uniform(own_keys[3], (TOKENS, TOP), jnp.float32) ** level_of(own_keys[3], (TOKENS, TOP), ((0, 16),), -0.2, 0.2)), 0.05, 0.5)
    gate_up = centred(own_keys[4], (EXPERTS, 2, HIDDEN_SIZE, D), D ** -0.5, 0.125, ((0, 16),))
    down_proj = centred(own_keys[5], (EXPERTS, HIDDEN_SIZE, D), HIDDEN_SIZE ** -0.5, 0.3125, ((0, 16),))
    owner_before = jax.random.permutation(own_keys[6], EXPERTS).astype(jnp.int32)
    migrating = draw_migrating(jax.random.fold_in(jax.random.fold_in(arg_keys[8], part), 71), part)
    return {"saved_inputs": saved_inputs, "out_grads": out_grads, "expert_ids": expert_ids, "gate_weights": gate_weights, "gate_up": gate_up, "down_proj": down_proj, "owner_before": owner_before, "migrating": migrating}


def silu_parts(values):
    sig = jax.nn.sigmoid(values)
    return values * sig, sig * (1.0 + values * (1.0 - sig))


def inverse_of(perm):
    count = perm.shape[0]
    return jnp.zeros((count,), jnp.int32).at[perm].set(jnp.arange(count, dtype=jnp.int32))


def reference(saved_inputs, out_grads, expert_ids, gate_weights, gate_up, down_proj, owner_before, migrating):
    owner_after = owner_before.at[migrating].set(owner_before[jnp.roll(migrating, -1)])
    flat_ids = expert_ids.reshape(-1)
    limit = TOKENS * TOP
    rows_max = N_EP * CAP
    group = HIDDEN_SIZE // N_MEM
    flat_gates = jnp.concatenate([gate_weights.reshape(-1), jnp.zeros((1,), jnp.float32)])
    inputs_ext = jnp.concatenate([saved_inputs, jnp.zeros((1, D), jnp.bfloat16)], 0)
    grads_ext = jnp.concatenate([out_grads, jnp.zeros((1, D), jnp.bfloat16)], 0)

    def one_expert(total, expert):
        slot = owner_before[expert]
        w_gate = gate_up[slot, 0]
        w_up = gate_up[slot, 1]
        w_down = down_proj[slot]
        chosen = jnp.nonzero(flat_ids == expert, size=rows_max, fill_value=limit)[0].astype(jnp.int32)
        token = chosen // TOP
        rows_in = inputs_ext[token]
        cot = (flat_gates[chosen][:, None] * grads_ext[token].astype(jnp.float32)).astype(jnp.bfloat16)
        pre_a = jnp.dot(rows_in, w_gate.T, preferred_element_type=jnp.float32)
        pre_b = jnp.dot(rows_in, w_up.T, preferred_element_type=jnp.float32)
        act, dact = silu_parts(pre_a)
        hidden = (act * pre_b).astype(jnp.bfloat16)
        d_hidden = jnp.dot(cot, w_down.T, preferred_element_type=jnp.float32)
        grad_a = (d_hidden * pre_b * dact).astype(jnp.bfloat16)
        grad_b = (d_hidden * act).astype(jnp.bfloat16)
        g_gate = jnp.dot(grad_a.T, rows_in, preferred_element_type=jnp.float32)
        g_up = jnp.dot(grad_b.T, rows_in, preferred_element_type=jnp.float32)
        g_down = jnp.dot(hidden.T, cot, preferred_element_type=jnp.float32)
        slot_sum = jnp.zeros((rows_max, D), jnp.float32)
        for index in range(N_MEM):
            low = index * group
            high = low + group
            partial_sum = jnp.dot(grad_a[:, low:high], w_gate[low:high], preferred_element_type=jnp.float32)
            partial_sum = partial_sum + jnp.dot(grad_b[:, low:high], w_up[low:high], preferred_element_type=jnp.float32)
            rounded = lax.optimization_barrier(partial_sum.astype(jnp.bfloat16))
            slot_sum = slot_sum + rounded.astype(jnp.float32)
        slot_grads = lax.optimization_barrier(slot_sum.astype(jnp.bfloat16))
        total = total.at[token].add(slot_grads.astype(jnp.float32))
        return total, (jnp.stack([g_gate, g_up]), g_down)

    start = jnp.zeros((TOKENS + 1, D), jnp.float32)
    total, (grads_gu, grads_down) = lax.scan(one_expert, start, jnp.arange(EXPERTS, dtype=jnp.int32))
    input_grads = total[:TOKENS].astype(jnp.bfloat16)
    inv_after = inverse_of(owner_after)
    source_slot = owner_before[inv_after]
    moved_gate_up = gate_up[source_slot]
    moved_down = down_proj[source_slot]
    return input_grads, moved_gate_up, moved_down, grads_gu[inv_after], grads_down[inv_after]
```

```python
import jax
import jax.numpy as jnp
from jax import lax
from jax.experimental import pallas as pl
from jax.sharding import PartitionSpec as P


def silu_parts(values):
    sig = jax.nn.sigmoid(values)
    return (values * sig, sig * (1.0 + values * (1.0 - sig)))


class Grid:
    def __init__(self, owners):
        self.ny = 2
        self.nc = 2
        self.nz = owners // 4
        self.me = lax.axis_index("ep")
        self.z = self.me // 4

    def spot(self, z, y, c):
        return (z * self.ny + y) * self.nc + c

    def hop(self, v, step, first, last):
        pairs = [
            (self.spot(z, y, c), self.spot(z + step, y, c))
            for z in range(first, last + 1)
            for y in range(self.ny)
            for c in range(self.nc)
        ]
        return lax.ppermute(v, "ep", pairs)

    def swap_y(self, v):
        pairs = [
            (self.spot(z, y, c), self.spot(z, 1 - y, c))
            for z in range(self.nz)
            for y in range(self.ny)
            for c in range(self.nc)
        ]
        return lax.ppermute(v, "ep", pairs)

    def swap_core(self, v):
        pairs = [
            (self.spot(z, y, c), self.spot(z, y, 1 - c))
            for z in range(self.nz)
            for y in range(self.ny)
            for c in range(self.nc)
        ]
        return lax.ppermute(v, "ep", pairs)

    def gather_line(self, v):
        nz = self.nz
        up, down = [v], [v]
        for s in range(1, nz):
            up.append(self.hop(up[-1], 1, s - 1, nz - 2))
            down.append(self.hop(down[-1], -1, 1, nz - s))
        return [v] + [jnp.where(self.z >= i, up[i], down[nz - i]) for i in range(1, nz)]

    def reduce_line(self, parts):
        nz = self.nz
        up = down = None
        for s in range(nz - 1, 0, -1):
            u = parts[nz - s] if up is None else parts[nz - s] + up
            d = parts[s] if down is None else parts[s] + down
            up = self.hop(u, 1, 0, nz - 1 - s)
            down = self.hop(d, -1, s, nz - 1)
        return parts[0] + up + down

    def order(self):
        z, y, c = self.me // 4, (self.me // 2) % 2, self.me % 2
        k = jnp.arange(2, dtype=jnp.int32)[:, None, None]
        j = jnp.arange(2, dtype=jnp.int32)[None, :, None]
        i = jnp.arange(self.nz, dtype=jnp.int32)[None, None, :]
        return (((z - i) % self.nz) * 4 + (y ^ j) * 2 + (c ^ k)).reshape(-1)


def gather_tokens(grid, x, g):
    width = x.shape[1]
    line = jnp.stack(grid.gather_line(x))
    x_own = jnp.stack([line, grid.swap_y(line)]).reshape(-1, width)
    pair = jnp.stack([g, grid.swap_y(g)])
    g_own = jnp.stack(grid.gather_line(pair), axis=1).reshape(-1, width)
    return [x_own, grid.swap_core(x_own)], [g_own, grid.swap_core(g_own)]


def scatter_tokens(grid, own, other, rows):
    width = own.shape[1]
    v = (own + grid.swap_core(other)).reshape(2, grid.nz, rows, width)
    half = width // 2
    lo = v[..., :half]
    hi = v[..., half:]
    lo = lo[0] + grid.swap_y(lo[1])
    lo = grid.reduce_line([lo[i] for i in range(grid.nz)])
    hi = grid.reduce_line([hi[:, i] for i in range(grid.nz)])
    hi = hi[0] + grid.swap_y(hi[1])
    return jnp.concatenate([lo, hi], axis=1)


def a2a(v):
    return lax.all_to_all(v, "ep", split_axis=0, concat_axis=0, tiled=True)


BY_LAST = (((1,), (1,)), ((), ()))
BY_ROW = (((0,), (0,)), ((), ()))


def matmul(a, b, dims=(((1,), (0,)), ((), ()))):
    return lax.dot_general(a, b, dims, preferred_element_type=jnp.float32)


def expert_terms(x, g, weight, pair, down):
    half = down.shape[0]
    both = matmul(x, pair, BY_LAST)
    pre_a, pre_b = both[:, :half], both[:, half:]
    cot = (weight * g.astype(jnp.float32)).astype(jnp.bfloat16)
    d_hidden = matmul(cot, down, BY_LAST)
    act, dact = silu_parts(pre_a)
    hidden = (act * pre_b).astype(jnp.bfloat16)
    d_pair = jnp.concatenate([d_hidden * pre_b * dact, d_hidden * act], 1).astype(jnp.bfloat16)
    return hidden, cot, d_pair


def row_block(tile, n):
    return pl.BlockSpec((tile, n), lambda i: (i, 0))


def whole_block(a):
    return pl.BlockSpec(a.shape, lambda i: (0, 0))


def tile_of(rows):
    return 512 if rows % 512 == 0 else rows


def input_side(x, g, weight, pair, down):
    rows, width = x.shape
    tile = tile_of(rows)

    def body(x, g, weight, pair, down, out):
        _, _, d_pair = expert_terms(x[...], g[...], weight[...], pair[...], down[...])
        out[...] = matmul(d_pair, pair[...]).astype(jnp.bfloat16)

    return pl.pallas_call(
        body,
        grid=(rows // tile,),
        in_specs=[row_block(tile, width)] * 2
        + [row_block(tile, 1), whole_block(pair), whole_block(down)],
        out_specs=row_block(tile, width),
        out_shape=jax.ShapeDtypeStruct((rows, width), jnp.bfloat16),
        name="input_side",
    )(x, g, weight, pair, down)


def weight_side(x, g, weight, pair, down):
    rows, width = x.shape
    tile = tile_of(rows)

    def body(x, g, weight, pair, down, pair_out, down_out):
        tokens = x[...]
        hidden, cot, d_pair = expert_terms(tokens, g[...], weight[...], pair[...], down[...])
        add_pair = matmul(d_pair, tokens, BY_ROW)
        add_down = matmul(hidden, cot, BY_ROW)

        @pl.when(pl.program_id(0) == 0)
        def _():
            pair_out[...] = add_pair
            down_out[...] = add_down

        @pl.when(pl.program_id(0) > 0)
        def _():
            pair_out[...] += add_pair
            down_out[...] += add_down

    return pl.pallas_call(
        body,
        grid=(rows // tile,),
        in_specs=[row_block(tile, width)] * 2
        + [row_block(tile, 1), whole_block(pair), whole_block(down)],
        out_specs=[whole_block(pair), whole_block(down)],
        out_shape=[
            jax.ShapeDtypeStruct(pair.shape, jnp.float32),
            jax.ShapeDtypeStruct(down.shape, jnp.float32),
        ],
        name="weight_side",
    )(x, g, weight, pair, down)


def local(x, g, expert_ids, gate_weights, gate_up, down_proj, owner_before, migrating):
    owners = lax.axis_size("ep")
    mem = lax.axis_size("mem")
    rows = x.shape[0]
    experts = owner_before.shape[0]
    half = down_proj.shape[1]
    width = down_proj.shape[2]
    names = jnp.arange(experts, dtype=jnp.int32)
    spots = jnp.arange(owners, dtype=jnp.int32)

    moves = migrating[:, None] == names[None, :]
    onward = jnp.sum(jnp.where(jnp.roll(moves, -1, axis=0), owner_before[None, :], 0), axis=1)
    owner_after = jnp.where(
        jnp.any(moves, axis=0), jnp.sum(jnp.where(moves, onward[:, None], 0), axis=0), owner_before
    )
    lands = owner_after[None, :] == spots[:, None]
    source_slot = jnp.sum(jnp.where(lands, owner_before[None, :], 0), axis=1)

    gate_of = jnp.sum(
        jnp.where(
            expert_ids.T[None, :, :] == names[:, None, None], gate_weights.T[None, :, :], 0.0
        ),
        axis=1,
    )
    begins = owner_before[None, :] == spots[:, None]
    gate_old = jnp.sum(jnp.where(begins[:, :, None], gate_of[None], 0.0), axis=1)
    gate_new = jnp.sum(jnp.where(lands[:, :, None], gate_of[None], 0.0), axis=1)
    gates = a2a(jnp.stack([gate_old, gate_new], axis=1))

    groups = 3 if half % (3 * owners) == 0 else 1
    hid = half // groups
    piece = hid // owners
    moved = []
    for n in range(groups):
        lo = n * hid
        pieces = jnp.concatenate(
            [
                gate_up[0, :, lo : lo + hid].reshape(2, owners, piece, width),
                down_proj[:, lo : lo + hid].reshape(1, owners, piece, width),
            ],
            axis=0,
        ).transpose(1, 0, 2, 3)
        spread = a2a(pieces.reshape(owners, 3 * piece, width))
        sent = jnp.take(spread, source_slot, axis=0)
        got = a2a(sent).reshape(owners, 3, piece, width)
        moved.append(got.transpose(1, 0, 2, 3).reshape(3, hid, width))

    w_pair, w_down = gate_up.reshape(2 * half, width), down_proj.reshape(half, width)
    if mem == 1 and owners == 16:
        grid = Grid(owners)
        x_all, g_all = gather_tokens(grid, x, g)
        gates = jnp.take(gates, grid.order(), axis=0).transpose(1, 0, 2).reshape(2, 2, -1, 1)
        own, other = (
            input_side(x_all[k], g_all[k], gates[0, k], w_pair, w_down) for k in range(2)
        )
        input_grads = scatter_tokens(grid, own, other, rows)
        x_all, g_all = jnp.concatenate(x_all), jnp.concatenate(g_all)
        weight_new = gates[1].reshape(-1, 1)
    else:
        x_all, g_all = (
            lax.all_gather(lax.all_gather(v, "ep", axis=0, tiled=True), "mem", axis=1, tiled=True)
            for v in (x, g)
        )
        gates = gates.transpose(1, 0, 2).reshape(2, -1, 1)
        dx = input_side(x_all, g_all, gates[0], w_pair, w_down)
        dx = lax.psum_scatter(dx, "mem", scatter_dimension=1, tiled=True)
        dx = lax.psum_scatter(dx.astype(jnp.float32), "ep", scatter_dimension=0, tiled=True)
        input_grads = dx.astype(jnp.bfloat16)
        weight_new = gates[1]

    grad_gate, grad_up, grad_down = [], [], []
    for block in moved:
        pair, down = weight_side(
            x_all, g_all, weight_new, block[:2].reshape(2 * hid, width), block[2]
        )
        grad_gate.append(pair[:hid])
        grad_up.append(pair[hid:])
        grad_down.append(down)
    moved = jnp.concatenate(moved, axis=1)
    return (
        input_grads,
        moved[:2].reshape(1, 2, half, width),
        moved[2:].reshape(1, half, width),
        jnp.concatenate(grad_gate + grad_up, axis=0).reshape(1, 2, half, width),
        jnp.concatenate(grad_down, axis=0).reshape(1, half, width),
    )


def solution(mesh):
    return jax.shard_map(
        local,
        mesh=mesh,
        in_specs=(
            P(("parts", "ep"), "mem"),
            P(("parts", "ep"), "mem"),
            P(("parts", "ep"), None),
            P(("parts", "ep"), None),
            P(("parts", "ep"), None, "mem", None),
            P(("parts", "ep"), "mem", None),
            P("parts"),
            P("parts"),
        ),
        out_specs=(
            P(("parts", "ep"), "mem"),
            P(("parts", "ep"), None, "mem", None),
            P(("parts", "ep"), "mem", None),
            P(("parts", "ep"), None, "mem", None),
            P(("parts", "ep"), "mem", None),
        ),
        check_vma=False,
    )
```
